32 devices in a mesh: dp: 8 (over z, y), tensor: 4 (over x, core).
Axes of the slice: x: 2, y: 2, z: 4, core: 2. Of those that a mesh axis runs over, the one named last changes fastest.
Arguments:
- query_tokens: float32 [2048, 768], P('dp'), may hold values from -6 to 6
- passage_tokens: float32 [6144, 768], P('dp'), may hold values from -6 to 6
- query_mask: int32 [64, 32], P('dp'), may hold values from 0 to 1, as said below
- passage_lengths: int32 [24], replicated, may hold values from 64 to 256, as said below
- positives: int32 [64], replicated, may hold values from 0 to 23
- qkv_weight: float32 [2, 3, 768, 768], P(None, None, 'dp', 'tensor'), may hold values from -0.21875 to 0.21875
- qkv_moment: float32 [2, 3, 768, 768], P(None, None, 'dp', 'tensor'), may hold values from -0.18 to 0.18
- qkv_second: float32 [2, 3, 768, 768], P(None, None, 'dp', 'tensor'), may hold values from 5e-05 to 0.0005
- out_weight: float32 [2, 768, 768], P(None, 'tensor', 'dp'), may hold values from -0.875 to 0.875
- out_moment: float32 [2, 768, 768], P(None, 'tensor', 'dp'), may hold values from -0.09 to 0.09
- out_second: float32 [2, 768, 768], P(None, 'tensor', 'dp'), may hold values from 7e-06 to 7e-05
- up_weight: float32 [2, 768, 3072], P(None, 'dp', 'tensor'), may hold values from -0.21875 to 0.21875
- up_moment: float32 [2, 768, 3072], P(None, 'dp', 'tensor'), may hold values from -0.12 to 0.12
- up_second: float32 [2, 768, 3072], P(None, 'dp', 'tensor'), may hold values from 1.5e-05 to 0.00015
- down_weight: float32 [2, 3072, 768], P(None, 'tensor', 'dp'), may hold values from -0.15625 to 0.15625
- down_moment: float32 [2, 3072, 768], P(None, 'tensor', 'dp'), may hold values from -0.15 to 0.15
- down_second: float32 [2, 3072, 768], P(None, 'tensor', 'dp'), may hold values from 3e-05 to 0.0003
- projection: float32 [768, 128], P('dp'), may hold values from -0.21875 to 0.21875
- projection_moment: float32 [768, 128], P('dp'), may hold values from -0.6 to 0.6
- projection_second: float32 [768, 128], P('dp'), may hold values from 0.0004 to 0.004
- bias_pair: float32 [2, 2, 768], P(None, None, 'tensor'), may hold values from -3 to 3
- bias_pair_moment: float32 [2, 2, 768], P(None, None, 'tensor'), may hold values from -0.36 to 0.36
- bias_pair_second: float32 [2, 2, 768], P(None, None, 'tensor'), may hold values from 0.0002 to 0.002
- bias_up: float32 [2, 3072], P(None, 'tensor'), may hold values from -3 to 3
- bias_up_moment: float32 [2, 3072], P(None, 'tensor'), may hold values from -0.072 to 0.072
- bias_up_second: float32 [2, 3072], P(None, 'tensor'), may hold values from 5e-06 to 5e-05
- norm_terms: float32 [2, 6, 768], replicated, may hold values from -2 to 2, as said below
- norm_terms_moment: float32 [2, 6, 768], replicated, may hold values from -0.18 to 0.18
- norm_terms_second: float32 [2, 6, 768], replicated, may hold values from 5e-05 to 0.0005
Outputs:
- loss_mean: float32 [], replicated
- query_grad: float32 [2048, 768], P(('dp', 'tensor'))
- passage_grad: float32 [6144, 768], P(('dp', 'tensor'))
- qkv_grad: float32 [2, 3, 768, 768], P(None, None, 'dp', 'tensor')
- qkv_moment_new: float32 [2, 3, 768, 768], P(None, None, 'dp', 'tensor')
- qkv_second_new: float32 [2, 3, 768, 768], P(None, None, 'dp', 'tensor')
- qkv_update: float32 [2, 3, 768, 768], P(None, None, 'dp', 'tensor')
- out_grad: float32 [2, 768, 768], P(None, 'tensor', 'dp')
- out_moment_new: float32 [2, 768, 768], P(None, 'tensor', 'dp')
- out_second_new: float32 [2, 768, 768], P(None, 'tensor', 'dp')
- out_update: float32 [2, 768, 768], P(None, 'tensor', 'dp')
- up_grad: float32 [2, 768, 3072], P(None, 'dp', 'tensor')
- up_moment_new: float32 [2, 768, 3072], P(None, 'dp', 'tensor')
- up_second_new: float32 [2, 768, 3072], P(None, 'dp', 'tensor')
- up_update: float32 [2, 768, 3072], P(None, 'dp', 'tensor')
- down_grad: float32 [2, 3072, 768], P(None, 'tensor', 'dp')
- down_moment_new: float32 [2, 3072, 768], P(None, 'tensor', 'dp')
- down_second_new: float32 [2, 3072, 768], P(None, 'tensor', 'dp')
- down_update: float32 [2, 3072, 768], P(None, 'tensor', 'dp')
- projection_grad: float32 [768, 128], P('dp')
- projection_moment_new: float32 [768, 128], P('dp')
- projection_second_new: float32 [768, 128], P('dp')
- projection_update: float32 [768, 128], P('dp')
- bias_pair_grad: float32 [2, 2, 768], P(None, None, 'tensor')
- bias_pair_moment_new: float32 [2, 2, 768], P(None, None, 'tensor')
- bias_pair_second_new: float32 [2, 2, 768], P(None, None, 'tensor')
- bias_pair_update: float32 [2, 2, 768], P(None, None, 'tensor')
- bias_up_grad: float32 [2, 3072], P(None, 'tensor')
- bias_up_moment_new: float32 [2, 3072], P(None, 'tensor')
- bias_up_second_new: float32 [2, 3072], P(None, 'tensor')
- bias_up_update: float32 [2, 3072], P(None, 'tensor')
- norm_terms_grad: float32 [2, 6, 768], replicated
- norm_terms_moment_new: float32 [2, 6, 768], replicated
- norm_terms_second_new: float32 [2, 6, 768], replicated
- norm_terms_update: float32 [2, 6, 768], replicated
The draws below stay inside these ranges and needn't reach their ends.
Inputs may be any that keep to these rules, and one draw needn't show every extreme that they name: `query_mask`: each row holds ones at its first 4 to 32 positions and zeros after them; some row is all ones. `passage_lengths`: some passage has all 256 tokens. `norm_terms`: rows 1 and 4 of each layer are gains between 0.4 and 1.6; the other rows lie between -2 and 2.
All inputs are finite; a program needn't handle non-finite values.
Results may differ from the reference program's by a relative error of at most 0.034.
Values may be sent and summed in bfloat16 or wider, within the bound.
No kernel may reach another device: no remote copies, remote signals or barrier semaphores. Data moves between devices by JAX's collectives and lax.ppermute only.
A program may use at most 192 MiB of HBM per device.

```python
import math
import jax
import jax.numpy as jnp
from jax import lax

D = 768
HEAD = 64
FF = 3072
DIM = 128
QLEN = 32
PLEN = 256
LAYERS = 2
STEP = 10
QDEV = 8
QUERIES = 64
PASSAGES = 24


def draw_query_mask(key, part):
    counts = jax.random.randint(jax.random.fold_in(key, 11), (QUERIES,), 4, QLEN + 1)
    longest = jax.random.randint(jax.random.fold_in(key, 12), (), 0, QUERIES)
    counts = jnp.where(jnp.arange(QUERIES) == longest, QLEN, counts)
    return (jnp.arange(QLEN)[None, :] < counts[:, None]).astype(jnp.int32)


def draw_passage_lengths(key, part):
    counts = jax.random.randint(jax.random.fold_in(key, 21), (PASSAGES,), PLEN // 4, PLEN + 1)
    longest = jax.random.randint(jax.random.fold_in(key, 22), (), 0, PASSAGES)
    return jnp.where(jnp.arange(PASSAGES) == longest, PLEN, counts).astype(jnp.int32)


def draw_norm_terms(key, part):
    base = jnp.clip(jax.random.normal(key, (LAYERS, 6, D), jnp.float32), -4.0, 4.0)
    row_index = lax.broadcasted_iota(jnp.int32, (LAYERS, 6, D), 1)
    gain_rows = (row_index == 1) | (row_index == 4)
    return jnp.where(gain_rows, 1.0 + 0.15 * base, 0.5 * base).astype(jnp.float32)


def set_ends(drawn, key, least, top_value):
    longest = drawn.shape.index(max(drawn.shape))
    spots = []
    for shift in (0, 1):
        where = [jax.random.randint(jax.random.fold_in(key, axis), (), 0, length) for axis, length in enumerate(drawn.shape)]
        where[longest] = (where[longest] + shift) % drawn.shape[longest]
        spots.append(tuple(where))
    return drawn.at[spots[0]].set(least).at[spots[1]].set(top_value)


def block_scale(rng, shape, pieces, low, high):
    gain, own = 1.0, jax.random.fold_in(rng, 6)
    for position, shards_of in pieces:
        heights = jnp.exp(jax.random.uniform(jax.random.fold_in(own, position), (shards_of,), jnp.float32, low / len(pieces), high / len(pieces)))
        gain = gain * jnp.repeat(heights, shape[position] // shards_of).reshape([-1 if axis == position else 1 for axis in range(len(shape))])
    return gain


def bell_draw(key, extent, deviation, bound, cuts=(), kind=jnp.bfloat16):
    drawn = jax.random.normal(key, extent, jnp.float32) * deviation
    if len(cuts) > 0:
        drawn = block_scale(key, extent, cuts, -0.22, 0.18) * drawn
    return jnp.clip(drawn, min=-bound, max=bound).astype(kind)


def setup_inputs(seed: int = 0) -> dict:
    key_list = jax.random.split(jax.random.key(seed), 30)
    query_tokens = bell_draw(key_list[0], (QUERIES * QLEN, D), 1.0, 6.0, ((0, 8),), jnp.float32)
    passage_tokens = bell_draw(key_list[1], (PASSAGES * PLEN, D), 1.0, 6.0, ((0, 8),), jnp.float32)
    query_mask = draw_query_mask(jax.random.fold_in(key_list[29], 71), 0)
    passage_lengths = draw_passage_lengths(jax.random.fold_in(key_list[29], 71), 0)
    positives = set_ends(jax.random.randint(key_list[4], (QUERIES,), 0, PASSAGES), jax.random.fold_in(key_list[4], 1), 0, PASSAGES - 1).astype(jnp.int32)
    qkv_weight = bell_draw(key_list[5], (LAYERS, 3, D, D), D ** -0.5, 0.21875, ((2, 8), (3, 4)), jnp.float32)
    qkv_moment = bell_draw(key_list[6], (LAYERS, 3, D, D), 0.03, 0.18, ((2, 8), (3, 4)), jnp.float32)
    qkv_second = jnp.clip(jnp.exp(math.log(0.0005) - 2.3025852 * jax.random.uniform(key_list[7], (LAYERS, 3, D, D), jnp.float32) ** block_scale(key_list[7], (LAYERS, 3, D, D), ((2, 8), (3, 4)), -0.2, 0.2)), 4.999999873689376e-05, 0.0005)
    out_weight = bell_draw(key_list[8], (LAYERS, D, D), (D // 16) ** -0.5, 0.875, ((1, 4), (2, 8)), jnp.float32)
    out_moment = bell_draw(key_list[9], (LAYERS, D, D), 0.015, 0.09, ((1, 4), (2, 8)), jnp.float32)
    out_second = jnp.clip(jnp.exp(math.log(7.000000186963007e-05) - 2.3025851 * jax.random.uniform(key_list[10], (LAYERS, D, D), jnp.float32) ** block_scale(key_list[10], (LAYERS, D, D), ((1, 4), (2, 8)), -0.2, 0.2)), 7.000000096013537e-06, 7.000000186963007e-05)
    up_weight = bell_draw(key_list[11], (LAYERS, D, FF), D ** -0.5, 0.21875, ((1, 8), (2, 4)), jnp.float32)
    up_moment = bell_draw(key_list[12], (LAYERS, D, FF), 0.02, 0.12, ((1, 8), (2, 4)), jnp.float32)
    up_second = jnp.clip(jnp.exp(math.log(0.00015) - 2.3025852 * jax.random.uniform(key_list[13], (LAYERS, D, FF), jnp.float32) ** block_scale(key_list[13], (LAYERS, D, FF), ((1, 8), (2, 4)), -0.2, 0.2)), 1.4999999621068127e-05, 0.00015)
    down_weight = bell_draw(key_list[14], (LAYERS, FF, D), (FF // 2) ** -0.5, 0.15625, ((1, 4), (2, 8)), jnp.float32)
    down_moment = bell_draw(key_list[15], (LAYERS, FF, D), 0.025, 0.15, ((1, 4), (2, 8)), jnp.float32)
    down_second = jnp.clip(jnp.exp(math.log(0.0003) - 2.3025852 * jax.random.uniform(key_list[16], (LAYERS, FF, D), jnp.float32) ** block_scale(key_list[16], (LAYERS, FF, D), ((1, 4), (2, 8)), -0.2, 0.2)), 2.9999999242136255e-05, 0.0003)
    projection = bell_draw(key_list[17], (D, DIM), D ** -0.5, 0.21875, ((0, 8),), jnp.float32)
    projection_moment = bell_draw(key_list[18], (D, DIM), 0.1, 0.6, ((0, 8),), jnp.float32)
    projection_second = jnp.clip(jnp.exp(math.log(0.004) - 2.3025852 * jax.random.uniform(key_list[19], (D, DIM), jnp.float32) ** block_scale(key_list[19], (D, DIM), ((0, 8),), -0.2, 0.2)), 0.0004, 0.004)
    bias_pair = bell_draw(key_list[20], (LAYERS, 2, D), 0.5, 3.0, ((2, 4),), jnp.float32)
    bias_pair_moment = bell_draw(key_list[21], (LAYERS, 2, D), 0.06, 0.36, ((2, 4),), jnp.float32)
    bias_pair_second = jnp.clip(jnp.exp(math.log(0.002) - 2.3025852 * jax.random.uniform(key_list[22], (LAYERS, 2, D), jnp.float32) ** block_scale(key_list[22], (LAYERS, 2, D), ((2, 4),), -0.2, 0.2)), 0.0002, 0.002)
    bias_up = bell_draw(key_list[23], (LAYERS, FF), 0.5, 3.0, ((1, 4),), jnp.float32)
    bias_up_moment = bell_draw(key_list[24], (LAYERS, FF), 0.012, 0.072, ((1, 4),), jnp.float32)
    bias_up_second = jnp.clip(jnp.exp(math.log(4.999999873689376e-05) - 2.3025851 * jax.random.uniform(key_list[25], (LAYERS, FF), jnp.float32) ** block_scale(key_list[25], (LAYERS, FF), ((1, 4),), -0.2, 0.2)), 4.999999873689376e-06, 4.999999873689376e-05)
    norm_terms = draw_norm_terms(jax.random.fold_in(key_list[29], 71), 0)
    norm_terms_moment = bell_draw(key_list[27], (LAYERS, 6, D), 0.03, 0.18, (), jnp.float32)
    norm_terms_second = jnp.clip(jnp.exp(jax.random.uniform(key_list[28], (LAYERS, 6, D), jnp.float32, math.log(4.999999873689376e-05), math.log(0.0005))), 4.999999873689376e-05, 0.0005)
    return {"query_tokens": query_tokens, "passage_tokens": passage_tokens, "query_mask": query_mask, "passage_lengths": passage_lengths, "positives": positives, "qkv_weight": qkv_weight, "qkv_moment": qkv_moment, "qkv_second": qkv_second, "out_weight": out_weight, "out_moment": out_moment, "out_second": out_second, "up_weight": up_weight, "up_moment": up_moment, "up_second": up_second, "down_weight": down_weight, "down_moment": down_moment, "down_second": down_second, "projection": projection, "projection_moment": projection_moment, "projection_second": projection_second, "bias_pair": bias_pair, "bias_pair_moment": bias_pair_moment, "bias_pair_second": bias_pair_second, "bias_up": bias_up, "bias_up_moment": bias_up_moment, "bias_up_second": bias_up_second, "norm_terms": norm_terms, "norm_terms_moment": norm_terms_moment, "norm_terms_second": norm_terms_second}


@jax.custom_vjp
def low(v):
    return lax.optimization_barrier(v.astype(jnp.bfloat16)).astype(jnp.float32)

@jax.custom_vjp
def low_back(v):
    return v

def low_keep(v):
    return (low(v), None)

def low_pass(kept, grad):
    return (grad,)

def back_keep(v):
    return (v, None)

def back_low(kept, grad):
    return (low(grad),)
low.defvjp(low_keep, low_pass)
low_back.defvjp(back_keep, back_low)
MASKED = -1e+30
SHARPNESS = 24.0
SCORE_SCALE = 4.0
LN_EPS = 1e-12
NORM_EPS = 1e-12
BETA_ONE = 0.9
BETA_TWO = 0.999
ADAM_EPS = 1e-08
LEARN_RATE = 0.02
WEIGHT_DECAY = 0.01
HIGHEST = lax.Precision.HIGHEST

def rounded_both(values):
    return low_back(low(values))

def matmul(left, right):
    return jnp.dot(left, right, precision=HIGHEST, preferred_element_type=jnp.float32)

def layer_norm(values, gains, shifts):
    average = lax.optimization_barrier(jnp.mean(values, -1, keepdims=True))
    centred = values - average
    factor = lax.rsqrt(lax.optimization_barrier(jnp.mean(centred * centred, -1, keepdims=True)) + LN_EPS)
    return centred * factor * gains + shifts

def encoder_layer(hidden, key_valid, qkv_low, out_low, up_low, down_low, bias_pair, bias_up, norm_terms):
    seq_count, length, width = hidden.shape
    row_data = hidden.reshape(seq_count * length, width)
    inputs = low(row_data)
    queries = rounded_both(matmul(inputs, qkv_low[0]) + bias_pair[0]).reshape(seq_count, length, -1, HEAD)
    keys_all = rounded_both(matmul(inputs, qkv_low[1])).reshape(seq_count, length, -1, HEAD)
    values = rounded_both(matmul(inputs, qkv_low[2]) + bias_pair[1]).reshape(seq_count, length, -1, HEAD)
    scores = low_back(jnp.einsum('sqhd,skhd->shqk', queries, keys_all, precision=HIGHEST) * 0.125)
    scores = jnp.where(key_valid[:, None, None, :], scores, MASKED)
    highest = lax.optimization_barrier(jnp.max(scores, -1, keepdims=True))
    powers = jnp.exp(scores - highest)
    chances = low(powers / lax.optimization_barrier(jnp.sum(powers, -1, keepdims=True)))
    mixture = jnp.einsum('shqk,skhd->sqhd', chances, values, precision=HIGHEST)
    mixture = rounded_both(mixture.reshape(seq_count * length, width))
    attended = low_back(matmul(mixture, out_low))
    first = layer_norm(row_data + attended + norm_terms[0], norm_terms[1], norm_terms[2])
    pre_act = low_back(matmul(low(first), up_low) + bias_up)
    spread = low_back(matmul(low(jax.nn.gelu(pre_act, approximate=False)), down_low))
    second = layer_norm(first + spread + norm_terms[3], norm_terms[4], norm_terms[5])
    return second.reshape(seq_count, length, width)

def embed(hidden, proj_low):
    seq_count, length, width = hidden.shape
    projected = low_back(matmul(low(hidden.reshape(seq_count * length, width)), proj_low))
    normed = projected * lax.rsqrt(lax.optimization_barrier(jnp.sum(projected * projected, -1, keepdims=True)) + NORM_EPS)
    return low(normed).reshape(seq_count, length, DIM)

def late_scores(query_block, passages, passage_valid, log_counts):
    similar = low_back(jnp.einsum('qid,pjd->qipj', query_block, passages, precision=HIGHEST))
    sharp = jnp.where(passage_valid[None, None], SHARPNESS * similar, MASKED)
    highest = lax.optimization_barrier(jnp.max(sharp, -1, keepdims=True))
    summed = lax.optimization_barrier(jnp.sum(jnp.exp(sharp - highest), -1))
    smooth = (highest[..., 0] + jnp.log(summed) - log_counts[None, None, :]) / SHARPNESS
    return SCORE_SCALE * lax.optimization_barrier(jnp.sum(smooth, 1))

def objective(qkv_weight, out_weight, up_weight, down_weight, projection, bias_pair, bias_up, norm_terms, query_tokens, passage_tokens, query_valid, passage_valid, log_counts, positives):
    qkv_low = low(qkv_weight)
    out_low = low(out_weight)
    up_low = low(up_weight)
    down_low = low(down_weight)
    queries = query_tokens.reshape(QUERIES, QLEN, D)
    passages = passage_tokens.reshape(PASSAGES, PLEN, D)
    for layer_at in range(LAYERS):
        queries = encoder_layer(queries, query_valid, qkv_low[layer_at], out_low[layer_at], up_low[layer_at], down_low[layer_at], bias_pair[layer_at], bias_up[layer_at], norm_terms[layer_at])
        passages = encoder_layer(passages, passage_valid, qkv_low[layer_at], out_low[layer_at], up_low[layer_at], down_low[layer_at], bias_pair[layer_at], bias_up[layer_at], norm_terms[layer_at])
    proj_low = low(projection)
    query_emb = embed(queries, proj_low)
    passage_emb = embed(passages, proj_low)
    blocks = query_emb.reshape(QUERIES // QDEV, QDEV, QLEN, DIM)
    scorer = jax.checkpoint(lambda block_in: late_scores(block_in, passage_emb, passage_valid, log_counts))
    logits = lax.map(scorer, blocks).reshape(QUERIES, PASSAGES)
    highest = lax.optimization_barrier(jnp.max(logits, -1, keepdims=True))
    log_total = highest[:, 0] + jnp.log(lax.optimization_barrier(jnp.sum(jnp.exp(logits - highest), -1)))
    chosen = jnp.arange(PASSAGES, dtype=jnp.int32)[None, :] == positives[:, None]
    picked = lax.optimization_barrier(jnp.sum(jnp.where(chosen, logits, 0.0), -1))
    return jnp.sum(log_total - picked)

def adam_step(master, moment, second, gradient, decay):
    moment_new = BETA_ONE * moment + (1.0 - BETA_ONE) * gradient
    second_new = BETA_TWO * second + (1.0 - BETA_TWO) * gradient * gradient
    rising = moment_new / (1.0 - BETA_ONE ** STEP)
    spread = jnp.sqrt(second_new / (1.0 - BETA_TWO ** STEP))
    return (moment_new, second_new, -LEARN_RATE * (rising / (spread + ADAM_EPS) + decay * master))

def reference(query_tokens, passage_tokens, query_mask, passage_lengths, positives, qkv_weight, qkv_moment, qkv_second, out_weight, out_moment, out_second, up_weight, up_moment, up_second, down_weight, down_moment, down_second, projection, projection_moment, projection_second, bias_pair, bias_pair_moment, bias_pair_second, bias_up, bias_up_moment, bias_up_second, norm_terms, norm_terms_moment, norm_terms_second):
    query_valid = query_mask == 1
    passage_valid = jnp.arange(PLEN, dtype=jnp.int32)[None, :] < passage_lengths[:, None]
    log_counts = jnp.log(passage_lengths.astype(jnp.float32))

    def closed(qkv_in, out_in, up_in, down_in, proj_in, pair_in, bias_in, norms_in, query_in, passage_in):
        return objective(qkv_in, out_in, up_in, down_in, proj_in, pair_in, bias_in, norms_in, query_in, passage_in, query_valid, passage_valid, log_counts, positives)
    total, pullback = jax.vjp(closed, qkv_weight, out_weight, up_weight, down_weight, projection, bias_pair, bias_up, norm_terms, query_tokens, passage_tokens)
    grads = pullback(jnp.ones_like(total))
    loss_mean = total / QUERIES
    qkv_m, qkv_v, qkv_u = adam_step(qkv_weight, qkv_moment, qkv_second, grads[0], WEIGHT_DECAY)
    out_m, out_v, out_u = adam_step(out_weight, out_moment, out_second, grads[1], WEIGHT_DECAY)
    up_m, up_v, up_u = adam_step(up_weight, up_moment, up_second, grads[2], WEIGHT_DECAY)
    down_m, down_v, down_u = adam_step(down_weight, down_moment, down_second, grads[3], WEIGHT_DECAY)
    proj_m, proj_v, proj_u = adam_step(projection, projection_moment, projection_second, grads[4], WEIGHT_DECAY)
    pair_m, pair_v, pair_u = adam_step(bias_pair, bias_pair_moment, bias_pair_second, grads[5], 0.0)
    bias_m, bias_v, bias_u = adam_step(bias_up, bias_up_moment, bias_up_second, grads[6], 0.0)
    norm_m, norm_v, norm_u = adam_step(norm_terms, norm_terms_moment, norm_terms_second, grads[7], 0.0)
    return (loss_mean, grads[8], grads[9], grads[0], qkv_m, qkv_v, qkv_u, grads[1], out_m, out_v, out_u, grads[2], up_m, up_v, up_u, grads[3], down_m, down_v, down_u, grads[4], proj_m, proj_v, proj_u, grads[5], pair_m, pair_v, pair_u, grads[6], bias_m, bias_v, bias_u, grads[7], norm_m, norm_v, norm_u)
```

```python
import functools

import jax
import jax.numpy as jnp
from jax import lax
from jax.experimental import pallas as pl
from jax.experimental.pallas import tpu as pltpu
from jax.sharding import PartitionSpec as P


HEAD = 64
DIM = 128
QLEN = 32
PLEN = 256
LAYERS = 2
STEP = 10
QDEV = 8
PDEV = 3
WIDE = 768
ROWS = 512
SEQ = 256
PART = 192
BF = jnp.bfloat16
F32 = jnp.float32

MASKED = -1e30
SHARPNESS = 24.0
SCORE_SCALE = 4.0
LN_EPS = 1e-12
NORM_EPS = 1e-12
BETA_ONE = 0.9
BETA_TWO = 0.999
ADAM_EPS = 1e-08
LEARN_RATE = 0.02
WEIGHT_DECAY = 0.01

VMEM_LIMIT = 48 * 1024 * 1024
ANY = pl.BlockSpec(memory_space=pl.ANY)


def swap(value, axis, bit):
    count = lax.axis_size(axis)
    return lax.ppermute(value, axis, [(i, i ^ bit) for i in range(count)])


def swap_core(value):
    return swap(value, "tensor", 1)


def swap_x(value):
    return swap(value, "tensor", 2)


def swap_y(value):
    return swap(value, "dp", 1)


def shift_z(value, by):
    return lax.ppermute(value, "dp", [(i, ((i // 2 + by) % 4) * 2 + i % 2) for i in range(8)])


KEYS = [(rx, ry, rz) for rx in (0, 1) for ry in (0, 1) for rz in range(4)]
PLAIN_KEYS = [(0, ry, rz) for ry in (0, 1) for rz in range(4)]


def gather_pieces(own, order, use_x=True):
    have = {(0, 0, 0): own}
    for axis in order:
        if axis == "x" and not use_x:
            continue
        for key in list(have):
            rx, ry, rz = key
            if axis == "x":
                have[(1, ry, rz)] = swap_x(have[key])
            elif axis == "y":
                have[(rx, 1, rz)] = swap_y(have[key])
            else:
                for by in (1, 2, 3):
                    have[(rx, ry, by)] = shift_z(have[key], by)
    return [have[key] for key in (KEYS if use_x else PLAIN_KEYS)]


def add_low(left, right):
    return (left.astype(F32) + right.astype(F32)).astype(BF)


def reduce_blocks(blocks, order):
    if order == "yx":
        low = {rx: add_low(blocks[(rx, 0)], swap_y(blocks[(rx, 1)])) for rx in (1, 0)}
        line = (low[0], swap_x(low[1]))
    else:
        low = {ry: add_low(blocks[(0, ry)], swap_x(blocks[(1, ry)])) for ry in (1, 0)}
        line = (low[0], swap_y(low[1]))
    pieces = [add_low(line[0][k], line[1][k]) for k in range(4)]
    total = pieces[0].astype(F32)
    for by in (1, 2, 3):
        total = total + shift_z(pieces[by], by).astype(F32)
    return total


def start_loads(info, refs, descs, target, sems):
    copies = []
    for at, (ref, desc) in enumerate(zip(refs, descs)):
        if len(desc) == 1:
            copy = pltpu.make_async_copy(ref, target.at[desc[0]], sems.at[at])
        else:
            (rx, ry, rz), from_row, count, shift = desc
            place = ((info[2] + 4 - rz) & 3) * 2 + (info[1] ^ ry)
            first = pl.multiple_of(place * 96 + shift, 16)
            copy = pltpu.make_async_copy(
                ref.at[pl.ds(from_row, count)], target.at[rx, pl.ds(first, count)], sems.at[at]
            )
        copies.append(copy)
    return copies


def norm_forward(values):
    average = jnp.mean(values, -1, keepdims=True)
    centred = values - average
    factor = lax.rsqrt(jnp.mean(centred * centred, -1, keepdims=True) + LN_EPS)
    return centred * factor, factor


def norm_backward(upstream, normal, factor, gains):
    scaled = upstream * gains
    average = jnp.mean(scaled, -1, keepdims=True)
    cross = jnp.mean(scaled * normal, -1, keepdims=True)
    return factor * (scaled - average - normal * cross)


def row_sum(values):
    return jnp.sum(values, 0, keepdims=True)


def dot(left, right):
    return jnp.dot(left, right, preferred_element_type=F32)


def dot_nt(left, right):
    return lax.dot_general(left, right, (((1,), (1,)), ((), ())), preferred_element_type=F32)


def widen(ref):
    return ref[...].astype(F32)


def erf_half(values):
    return 0.5 * (1.0 + lax.erf(values * 0.7071067811865476))


def attention_forward_kernel(descs, after_norm, info, *refs):
    refs = list(refs)
    pieces = [refs.pop(0) for _ in descs]
    if after_norm:
        first_ref, own_ref, peer_ref, norm_ref = [refs.pop(0) for _ in range(4)]
    else:
        x_in = refs.pop(0)
    bias_ref, mask_ref = refs.pop(0), refs.pop(0)
    both_ref, log_ref, xt_ref, part_ref = [refs.pop(0) for _ in range(4)]
    if after_norm:
        x_ref, normal_ref, factor_ref = [refs.pop(0) for _ in range(3)]
    held, sems = refs
    step = pl.program_id(0)

    @pl.when(step == 0)
    def _():
        for copy in start_loads(info, pieces, descs, held, sems):
            copy.start()

    if after_norm:
        added = first_ref[...] + (widen(own_ref) + widen(peer_ref)) + norm_ref[3:4]
        normal, factor = norm_forward(added)
        states = normal * norm_ref[4:5] + norm_ref[5:6]
        x_ref[...] = states
        normal_ref[...] = normal
        factor_ref[...] = jnp.broadcast_to(factor, (SEQ, 128))
    else:
        states = x_in[...]
    low = states.astype(BF)
    xt_ref[...] = states.T.astype(BF)

    @pl.when(step == 0)
    def _():
        for copy in start_loads(info, pieces, descs, held, sems):
            copy.wait()

    bias = mask_ref[0]
    total = None
    logs = []
    for rx in (0, 1):
        mixed = (dot(low, held[rx]) + bias_ref[rx : rx + 1]).astype(BF)
        values_t = mixed[:, 2 * PART : 3 * PART].T
        outs = []
        for head in range(3):
            queries = mixed[:, head * HEAD : (head + 1) * HEAD]
            keys = mixed[:, PART + head * HEAD : PART + (head + 1) * HEAD]
            scores = dot_nt(keys, queries) * 0.125 + bias
            highest = jnp.max(scores, 0, keepdims=True)
            powers = jnp.exp(scores - highest)
            summed = row_sum(powers)
            chances = (powers * (1.0 / summed)).astype(BF)
            outs.append(dot(values_t[head * HEAD : (head + 1) * HEAD], chances))
            logs.append(highest + jnp.log(summed))
        out = jnp.concatenate(outs, 0).T.astype(BF)
        both_ref[:, rx * WIDE : rx * WIDE + 3 * PART] = mixed[:, : 3 * PART]
        both_ref[:, rx * WIDE + 3 * PART : (rx + 1) * WIDE] = out
        term = dot_nt(out, held[rx, :, 3 * PART :])
        total = term if total is None else total + term
    part_ref[...] = total.astype(BF)
    log_ref[0] = jnp.concatenate(logs + [logs[0], logs[0]], 0)


def full(shape):
    return pl.BlockSpec(shape, lambda i, info: (0,) * len(shape))


def tile(shape, axis=0):
    def place(i, info):
        return tuple(i if at == axis else 0 for at in range(len(shape)))

    return pl.BlockSpec(shape, place)


def call(kernel, grid, info, inputs, in_specs, outs, out_specs, scratch, flops, name):
    moved = sum(v.size * v.dtype.itemsize for v in inputs) + sum(
        s.size * s.dtype.itemsize for s in outs
    )
    return pl.pallas_call(
        kernel,
        out_shape=outs,
        grid_spec=pltpu.PrefetchScalarGridSpec(
            num_scalar_prefetch=1,
            grid=grid,
            in_specs=in_specs,
            out_specs=out_specs,
            scratch_shapes=scratch,
        ),
        compiler_params=pltpu.CompilerParams(
            dimension_semantics=("arbitrary",) * len(grid), vmem_limit_bytes=VMEM_LIMIT
        ),
        cost_estimate=pl.CostEstimate(
            flops=int(flops), bytes_accessed=int(moved), transcendentals=0
        ),
        name=name,
    )(info, *inputs)


def shape_of(*dims, dtype=F32):
    return jax.ShapeDtypeStruct(dims, dtype)


def attention_forward(info, plane, states, normed, bias, masks):
    pieces, descs = plane
    inputs = list(pieces)
    in_specs = [ANY] * len(pieces)
    after_norm = normed is not None
    if after_norm:
        inputs += list(normed)
        in_specs += [tile((SEQ, WIDE))] * 3 + [full((6, WIDE))]
    else:
        inputs += [states]
        in_specs += [tile((SEQ, WIDE))]
    inputs += [bias, masks]
    in_specs += [full((2, WIDE)), tile((1, SEQ, SEQ))]
    outs = [
        shape_of(ROWS, 2 * WIDE, dtype=BF),
        shape_of(2, 8, SEQ),
        shape_of(WIDE, ROWS, dtype=BF),
        shape_of(ROWS, WIDE, dtype=BF),
    ]
    out_specs = [
        tile((SEQ, 2 * WIDE)),
        tile((1, 8, SEQ)),
        tile((WIDE, SEQ), 1),
        tile((SEQ, WIDE)),
    ]
    if after_norm:
        outs += [shape_of(ROWS, WIDE), shape_of(ROWS, WIDE), shape_of(ROWS, 128)]
        out_specs += [tile((SEQ, WIDE)), tile((SEQ, WIDE)), tile((SEQ, 128))]
    return call(
        functools.partial(attention_forward_kernel, descs, after_norm),
        (2,),
        info,
        inputs,
        in_specs,
        outs,
        out_specs,
        [pltpu.VMEM((2, WIDE, WIDE), BF), pltpu.SemaphoreType.DMA((len(descs),))],
        4e9,
        "attn_fwd",
    )


def hidden_forward_kernel(descs_up, descs_down, info, *refs):
    refs = list(refs)
    up_pieces = [refs.pop(0) for _ in descs_up]
    down_pieces = [refs.pop(0) for _ in descs_down]
    x_ref, own_ref, peer_ref, norm_ref, bias_ref = [refs.pop(0) for _ in range(5)]
    first_ref, normal_ref, factor_ref, first_t_ref, pre_ref, act_ref, part_ref = [
        refs.pop(0) for _ in range(7)
    ]
    up, down, up_sems, down_sems = refs
    step = pl.program_id(0)

    @pl.when(step == 0)
    def _():
        for copy in start_loads(info, up_pieces, descs_up, up, up_sems):
            copy.start()
        for copy in start_loads(info, down_pieces, descs_down, down, down_sems):
            copy.start()

    added = x_ref[...] + (widen(own_ref) + widen(peer_ref)) + norm_ref[0:1]
    normal, factor = norm_forward(added)
    first = normal * norm_ref[1:2] + norm_ref[2:3]
    first_ref[...] = first
    normal_ref[...] = normal
    factor_ref[...] = jnp.broadcast_to(factor, (SEQ, 128))
    low = first.astype(BF)
    first_t_ref[...] = first.T.astype(BF)

    @pl.when(step == 0)
    def _():
        for copy in start_loads(info, up_pieces, descs_up, up, up_sems):
            copy.wait()
        for copy in start_loads(info, down_pieces, descs_down, down, down_sems):
            copy.wait()

    total = None
    for rx in (0, 1):
        pre = dot(low, up[rx]) + bias_ref[rx : rx + 1]
        pre_ref[:, rx * WIDE : (rx + 1) * WIDE] = pre
        act = (pre * erf_half(pre)).astype(BF)
        act_ref[:, rx * WIDE : (rx + 1) * WIDE] = act
        term = dot_nt(act, down[rx])
        total = term if total is None else total + term
    part_ref[...] = total.astype(BF)


def hidden_forward(info, up, down, x, own, peer, norms, bias):
    inputs = list(up[0]) + list(down[0]) + [x, own, peer, norms, bias]
    in_specs = [ANY] * (len(up[0]) + len(down[0])) + [
        tile((SEQ, WIDE)),
        tile((SEQ, WIDE)),
        tile((SEQ, WIDE)),
        full((6, WIDE)),
        full((2, WIDE)),
    ]
    outs = [
        shape_of(ROWS, WIDE),
        shape_of(ROWS, WIDE),
        shape_of(ROWS, 128),
        shape_of(WIDE, ROWS, dtype=BF),
        shape_of(ROWS, 2 * WIDE),
        shape_of(ROWS, 2 * WIDE, dtype=BF),
        shape_of(ROWS, WIDE, dtype=BF),
    ]
    out_specs = [
        tile((SEQ, WIDE)),
        tile((SEQ, WIDE)),
        tile((SEQ, 128)),
        tile((WIDE, SEQ), 1),
        tile((SEQ, 2 * WIDE)),
        tile((SEQ, 2 * WIDE)),
        tile((SEQ, WIDE)),
    ]
    return call(
        functools.partial(hidden_forward_kernel, up[1], down[1]),
        (2,),
        info,
        inputs,
        in_specs,
        outs,
        out_specs,
        [
            pltpu.VMEM((2, WIDE, WIDE), BF),
            pltpu.VMEM((2, WIDE, WIDE), BF),
            pltpu.SemaphoreType.DMA((len(up[1]),)),
            pltpu.SemaphoreType.DMA((len(down[1]),)),
        ],
        2.4e9 * 2,
        "ffn_fwd",
    )


def embed_kernel(descs, info, *refs):
    refs = list(refs)
    pieces = [refs.pop(0) for _ in descs]
    first_ref, own_ref, peer_ref, norm_ref = [refs.pop(0) for _ in range(4)]
    normal_ref, factor_ref, xt_ref, embed_ref, low_ref, send_ref, proj_ref = [
        refs.pop(0) for _ in range(7)
    ]
    (sems,) = refs
    step = pl.program_id(0)

    @pl.when(step == 0)
    def _():
        for copy in start_loads(info, pieces, descs, proj_ref, sems):
            copy.start()

    added = first_ref[...] + (widen(own_ref) + widen(peer_ref)) + norm_ref[3:4]
    normal, factor = norm_forward(added)
    states = normal * norm_ref[4:5] + norm_ref[5:6]
    normal_ref[...] = normal
    factor_ref[...] = jnp.broadcast_to(factor, (SEQ, 128))
    xt_ref[...] = states.T.astype(BF)

    @pl.when(step == 0)
    def _():
        for copy in start_loads(info, pieces, descs, proj_ref, sems):
            copy.wait()

    embedded = dot(states.astype(BF), proj_ref[0])
    scale = lax.rsqrt(jnp.sum(embedded * embedded, -1, keepdims=True) + NORM_EPS)
    embed_ref[...] = embedded
    unit = (embedded * scale).astype(BF)
    low_ref[...] = unit

    @pl.when(step == info[3])
    def _():
        send_ref[...] = unit


def embed(info, proj, first, own, peer, norms):
    return call(
        functools.partial(embed_kernel, proj[1]),
        (2,),
        info,
        list(proj[0]) + [first, own, peer, norms],
        [ANY] * len(proj[0]) + [tile((SEQ, WIDE))] * 3 + [full((6, WIDE))],
        [
            shape_of(ROWS, WIDE),
            shape_of(ROWS, 128),
            shape_of(WIDE, ROWS, dtype=BF),
            shape_of(ROWS, DIM),
            shape_of(ROWS, DIM, dtype=BF),
            shape_of(SEQ, DIM, dtype=BF),
            shape_of(1, WIDE, DIM, dtype=BF),
        ],
        [
            tile((SEQ, WIDE)),
            tile((SEQ, 128)),
            tile((WIDE, SEQ), 1),
            tile((SEQ, DIM)),
            tile((SEQ, DIM)),
            full((SEQ, DIM)),
            full((1, WIDE, DIM)),
        ],
        [pltpu.SemaphoreType.DMA((len(proj[1]),))],
        2 * 512 * 768 * 128,
        "embed",
    )


def lay_out_kernel(count, info, *refs):
    pieces, out_ref, sems = refs[: 2 * count], refs[2 * count], refs[2 * count + 1]
    copies = []
    for half in (0, 1):
        for at, (rx, ry, rz) in enumerate(KEYS):
            place = ((info[2] + 4 - rz) & 3) * 2 + (info[1] ^ ry)
            copies.append(
                pltpu.make_async_copy(
                    pieces[half * count + at],
                    out_ref.at[info[0] ^ rx, place, pl.ds(half * 128, 128)],
                    sems.at[half * count + at],
                )
            )
    for copy in copies:
        copy.start()
    for copy in copies:
        copy.wait()


def lay_out(info, pieces):
    count = len(KEYS)
    return call(
        functools.partial(lay_out_kernel, count),
        (1,),
        info,
        pieces,
        [ANY] * len(pieces),
        [shape_of(2, 8, SEQ, DIM, dtype=BF)],
        [full((2, 8, SEQ, DIM))],
        [pltpu.SemaphoreType.DMA((2 * count,))],
        1e6,
        "lay_out",
    )[0]


def masked_powers(passage, queries, length):
    similar = dot_nt(passage, queries)
    position = lax.broadcasted_iota(jnp.int32, similar.shape, 0)
    return jnp.where(position < length, jnp.exp(SHARPNESS * similar), 0.0)


def score_kernel(passages, blocks, info, lengths, own_ref, peer_ref, all_ref, sum_ref, sems):
    core = info[3]
    copies = []
    for at in (0, 1):
        copies.append(
            pltpu.make_async_copy(own_ref.at[at], all_ref.at[at, core], sems.at[2 * at])
        )
        copies.append(
            pltpu.make_async_copy(peer_ref.at[at], all_ref.at[at, 1 - core], sems.at[2 * at + 1])
        )
    for copy in copies:
        copy.start()
    for copy in copies:
        copy.wait()
    first = info[5]

    def advance(at, carry):
        kind = at % PDEV + 1
        passage = all_ref[kind // 2, kind % 2, at // PDEV]
        length = lengths[at]
        for block in range(blocks):
            powers = masked_powers(passage, all_ref[0, 0, first + block], length)
            sum_ref[pl.ds(at, 1), block * SEQ : (block + 1) * SEQ] = row_sum(powers)
        return carry

    lax.fori_loop(0, passages, advance, 0)


def score(info, lengths, own, peer, blocks):
    passages = lengths.shape[0]
    groups = own.shape[1]
    outs = [
        shape_of(2, 2, groups, SEQ, DIM, dtype=BF),
        shape_of(passages, blocks * SEQ),
    ]
    return pl.pallas_call(
        functools.partial(score_kernel, passages, blocks),
        out_shape=outs,
        grid_spec=pltpu.PrefetchScalarGridSpec(
            num_scalar_prefetch=2,
            grid=(),
            in_specs=[ANY, ANY],
            out_specs=[
                pl.BlockSpec(memory_space=pltpu.VMEM),
                pl.BlockSpec(memory_space=pltpu.VMEM),
            ],
            scratch_shapes=[pltpu.SemaphoreType.DMA((4,))],
        ),
        compiler_params=pltpu.CompilerParams(vmem_limit_bytes=VMEM_LIMIT),
        cost_estimate=pl.CostEstimate(
            flops=int(passages * blocks * 2e7), bytes_accessed=4000000, transcendentals=0
        ),
        name="score",
    )(info, lengths, own, peer)


def score_back_kernel(passages, groups, info, lengths, *refs):
    (all_ref, steer_ref, embed_ref, xt_ref, proj_ref, upstream_ref, out_ref, dn_ref) = refs
    which_x, group = info[0], info[4]

    def weights_of(passage, queries, at, first):
        powers = masked_powers(passage, queries, lengths[at])
        first = pl.multiple_of(first, SEQ)
        pull = steer_ref[pl.ds(at, 1), pl.ds(first, SEQ)]
        return (powers * (pull / row_sum(powers))).astype(BF)

    def passage_side(slot, kind):
        passage = all_ref[kind // 2, kind % 2, group]
        at = group * PDEV + kind - 1
        dn_ref[slot * SEQ : (slot + 1) * SEQ] = jnp.zeros((SEQ, DIM), F32)

        def advance(block, carry):
            queries = all_ref[0, 0, block]
            shares = weights_of(passage, queries, at, block * SEQ)
            dn_ref[slot * SEQ : (slot + 1) * SEQ] += dot(shares, queries)
            return carry

        lax.fori_loop(0, groups, advance, 0)

    passage_side(1, 2 * which_x + 1)

    @pl.when(which_x == 1)
    def _():
        passage_side(0, 2)

    @pl.when(which_x == 0)
    def _():
        queries = all_ref[0, 0, group]
        dn_ref[:SEQ] = jnp.zeros((SEQ, DIM), F32)

        def advance(at, carry):
            kind = at % PDEV + 1
            passage = all_ref[kind // 2, kind % 2, at // PDEV]
            shares = weights_of(passage, queries, at, group * SEQ)
            dn_ref[:SEQ] += lax.dot_general(
                shares, passage, (((0,), (0,)), ((), ())), preferred_element_type=F32
            )
            return carry

        lax.fori_loop(0, passages, advance, 0)

    embedded = embed_ref[...]
    factor = lax.rsqrt(jnp.sum(embedded * embedded, -1, keepdims=True) + NORM_EPS)
    unit = embedded * factor
    grad = dn_ref[...]
    grad_low = (factor * (grad - unit * jnp.sum(grad * unit, -1, keepdims=True))).astype(BF)
    upstream_ref[...] = dot_nt(grad_low, proj_ref[0])
    out_ref[...] = dot(xt_ref[...], grad_low)


def score_back(info, lengths, everything, steer, embedded, xt, proj):
    passages, groups = lengths.shape[0], everything.shape[2]
    vmem = pl.BlockSpec(memory_space=pltpu.VMEM)
    return pl.pallas_call(
        functools.partial(score_back_kernel, passages, groups),
        out_shape=[shape_of(ROWS, WIDE), shape_of(WIDE, DIM)],
        grid_spec=pltpu.PrefetchScalarGridSpec(
            num_scalar_prefetch=2,
            grid=(),
            in_specs=[vmem] * 5,
            out_specs=[vmem, vmem],
            scratch_shapes=[pltpu.VMEM((ROWS, DIM), F32)],
        ),
        compiler_params=pltpu.CompilerParams(vmem_limit_bytes=VMEM_LIMIT),
        cost_estimate=pl.CostEstimate(flops=int(2e9), bytes_accessed=6000000, transcendentals=0),
        name="score_back",
    )(info, lengths, everything, steer, embedded, xt, proj)


def hidden_backward_kernel(descs_up, descs_down, terms, info, *refs):
    refs = list(refs)
    up_pieces = [refs.pop(0) for _ in descs_up]
    down_pieces = [refs.pop(0) for _ in descs_down]
    upstream_refs = [refs.pop(0) for _ in range(terms)]
    normal_ref, factor_ref, norm_ref, pre_ref = [refs.pop(0) for _ in range(4)]
    grad_ref, low_t_ref, pre_low_ref, part_ref, vec_ref = [refs.pop(0) for _ in range(5)]
    up, down, up_sems, down_sems = refs
    step = pl.program_id(0)

    @pl.when(step == 0)
    def _():
        for copy in start_loads(info, down_pieces, descs_down, down, down_sems):
            copy.start()
        for copy in start_loads(info, up_pieces, descs_up, up, up_sems):
            copy.start()
        vec_ref[...] = jnp.zeros((8, WIDE), F32)

    upstream = upstream_refs[0][...]
    if terms == 3:
        upstream = upstream + (widen(upstream_refs[1]) + widen(upstream_refs[2]))
    normal = normal_ref[...]
    grad = norm_backward(upstream, normal, factor_ref[:, :1], norm_ref[4:5])
    grad_ref[...] = grad
    low = grad.astype(BF)
    low_t_ref[...] = grad.T.astype(BF)
    vec_ref[0:1] += row_sum(upstream * normal)
    vec_ref[1:2] += row_sum(upstream)
    vec_ref[2:3] += row_sum(grad)

    @pl.when(step == 0)
    def _():
        for copy in start_loads(info, down_pieces, descs_down, down, down_sems):
            copy.wait()
        for copy in start_loads(info, up_pieces, descs_up, up, up_sems):
            copy.wait()

    total = None
    for rx in (0, 1):
        pre = pre_ref[:, rx * WIDE : (rx + 1) * WIDE]
        slope = erf_half(pre) + pre * jnp.exp(-0.5 * pre * pre) * 0.3989422804014327
        pre_low = (dot(low, down[rx]) * slope).astype(BF)
        pre_low_ref[:, rx * WIDE : (rx + 1) * WIDE] = pre_low
        vec_ref[3 + rx : 4 + rx] += row_sum(pre_low.astype(F32))
        term = dot_nt(pre_low, up[rx])
        total = term if total is None else total + term
    part_ref[...] = total.astype(BF)


def hidden_backward(info, up, down, upstream, normal, factor, norms, pre):
    inputs = list(up[0]) + list(down[0]) + list(upstream) + [normal, factor, norms, pre]
    in_specs = (
        [ANY] * (len(up[0]) + len(down[0]))
        + [tile((SEQ, WIDE))] * len(upstream)
        + [tile((SEQ, WIDE)), tile((SEQ, 128)), full((6, WIDE)), tile((SEQ, 2 * WIDE))]
    )
    return call(
        functools.partial(hidden_backward_kernel, up[1], down[1], len(upstream)),
        (2,),
        info,
        inputs,
        in_specs,
        [
            shape_of(ROWS, WIDE),
            shape_of(WIDE, ROWS, dtype=BF),
            shape_of(ROWS, 2 * WIDE, dtype=BF),
            shape_of(ROWS, WIDE, dtype=BF),
            shape_of(8, WIDE),
        ],
        [
            tile((SEQ, WIDE)),
            tile((WIDE, SEQ), 1),
            tile((SEQ, 2 * WIDE)),
            tile((SEQ, WIDE)),
            full((8, WIDE)),
        ],
        [
            pltpu.VMEM((2, WIDE, WIDE), BF),
            pltpu.VMEM((2, WIDE, WIDE), BF),
            pltpu.SemaphoreType.DMA((len(up[1]),)),
            pltpu.SemaphoreType.DMA((len(down[1]),)),
        ],
        5e9,
        "ffn_bwd",
    )


def attention_backward_kernel(descs, info, *refs):
    refs = list(refs)
    pieces = [refs.pop(0) for _ in descs]
    upstream_ref, own_ref, peer_ref, normal_ref, factor_ref, norm_ref = [
        refs.pop(0) for _ in range(6)
    ]
    both_ref, log_ref, mask_ref = [refs.pop(0) for _ in range(3)]
    grad_ref, low_t_ref, mixed_ref, part_ref, vec_ref = [refs.pop(0) for _ in range(5)]
    held, sems = refs
    step = pl.program_id(0)

    @pl.when(step == 0)
    def _():
        for copy in start_loads(info, pieces, descs, held, sems):
            copy.start()
        vec_ref[...] = jnp.zeros((8, WIDE), F32)

    upstream = upstream_ref[...] + (widen(own_ref) + widen(peer_ref))
    normal = normal_ref[...]
    grad = norm_backward(upstream, normal, factor_ref[:, :1], norm_ref[1:2])
    grad_ref[...] = grad
    low = grad.astype(BF)
    low_t_ref[...] = grad.T.astype(BF)
    vec_ref[0:1] += row_sum(upstream * normal)
    vec_ref[1:2] += row_sum(upstream)
    vec_ref[2:3] += row_sum(grad)

    @pl.when(step == 0)
    def _():
        for copy in start_loads(info, pieces, descs, held, sems):
            copy.wait()

    bias = mask_ref[0]
    total = None
    for rx in (0, 1):
        mixed = both_ref[:, rx * WIDE : (rx + 1) * WIDE]
        out_grad = dot(low, held[rx, :, 3 * PART :]).astype(BF)
        keys_t = mixed[:, PART : 2 * PART].T
        queries_grad, keys_grad, values_grad = [], [], []
        for head in range(3):
            queries = mixed[:, head * HEAD : (head + 1) * HEAD]
            keys = mixed[:, PART + head * HEAD : PART + (head + 1) * HEAD]
            values = mixed[:, 2 * PART + head * HEAD : 2 * PART + (head + 1) * HEAD]
            above = out_grad[:, head * HEAD : (head + 1) * HEAD]
            scores = dot_nt(keys, queries) * 0.125 + bias
            at = rx * 3 + head
            chances = jnp.exp(scores - log_ref[0, at : at + 1])
            values_grad.append(dot(chances.astype(BF), above))
            grads = dot_nt(values, above)
            inner = row_sum(chances * grads)
            slopes = (chances * (grads - inner)).astype(BF)
            keys_grad.append(dot(slopes, queries) * 0.125)
            queries_grad.append(dot(keys_t[head * HEAD : (head + 1) * HEAD], slopes) * 0.125)
        packed = jnp.concatenate(
            [jnp.concatenate(queries_grad, 0).T]
            + keys_grad
            + values_grad
            + [jnp.zeros((SEQ, PART), F32)],
            1,
        ).astype(BF)
        mixed_ref[:, rx * WIDE : (rx + 1) * WIDE] = packed
        vec_ref[3 + rx : 4 + rx] += row_sum(packed.astype(F32))
        term = dot_nt(packed, held[rx])
        total = term if total is None else total + term
    part_ref[...] = total.astype(BF)


def attention_backward(info, plane, upstream, own, peer, normal, factor, norms, both, logs, masks):
    pieces, descs = plane
    inputs = list(pieces) + [upstream, own, peer, normal, factor, norms, both, logs, masks]
    in_specs = [ANY] * len(pieces) + [
        tile((SEQ, WIDE)),
        tile((SEQ, WIDE)),
        tile((SEQ, WIDE)),
        tile((SEQ, WIDE)),
        tile((SEQ, 128)),
        full((6, WIDE)),
        tile((SEQ, 2 * WIDE)),
        tile((1, 8, SEQ)),
        tile((1, SEQ, SEQ)),
    ]
    return call(
        functools.partial(attention_backward_kernel, descs),
        (2,),
        info,
        inputs,
        in_specs,
        [
            shape_of(ROWS, WIDE),
            shape_of(WIDE, ROWS, dtype=BF),
            shape_of(ROWS, 2 * WIDE, dtype=BF),
            shape_of(ROWS, WIDE, dtype=BF),
            shape_of(8, WIDE),
        ],
        [
            tile((SEQ, WIDE)),
            tile((WIDE, SEQ), 1),
            tile((SEQ, 2 * WIDE)),
            tile((SEQ, WIDE)),
            full((8, WIDE)),
        ],
        [pltpu.VMEM((2, WIDE, WIDE), BF), pltpu.SemaphoreType.DMA((len(descs),))],
        6e9,
        "attn_bwd",
    )


def weight_grad_kernel(second, spread, info, *refs):
    refs = list(refs)
    left_ref, right_ref = refs.pop(0), refs.pop(0)
    if second:
        left_two_ref, right_two_ref = refs.pop(0), refs.pop(0)
    for rx in (0, 1):
        columns = slice(rx * WIDE, (rx + 1) * WIDE)
        value = dot(left_ref[...], right_ref[:, columns])
        if second:
            value = jnp.concatenate(
                [
                    value[:, : 3 * PART],
                    dot(left_two_ref[...], right_two_ref[:, rx * WIDE + 3 * PART : (rx + 1) * WIDE]),
                ],
                1,
            )
        if spread:
            upper, lower = value[:96], value[96:]
            odd = info[1] == 1
            refs[2 * rx][0] = jnp.where(odd, lower, upper).astype(BF)
            refs[2 * rx + 1][0] = jnp.where(odd, upper, lower).astype(BF)
        else:
            refs[rx][...] = value.astype(BF)


def weight_grad(info, spread, left, right, second=None):
    inputs = [left, right] + list(second or ())
    one = [
        pl.BlockSpec((2 * 96, ROWS), lambda i, info: (i, 0)),
        full((ROWS, 2 * WIDE)),
    ]
    if spread:
        outs = [shape_of(4, 96, WIDE, dtype=BF)] * 4
        spec = pl.BlockSpec((1, 96, WIDE), lambda i, info: ((i + 4 - info[2]) & 3, 0, 0))
        out_specs = [spec] * 4
    else:
        outs = [shape_of(WIDE, WIDE, dtype=BF)] * 2
        out_specs = [pl.BlockSpec((2 * 96, WIDE), lambda i, info: (i, 0))] * 2
    got = call(
        functools.partial(weight_grad_kernel, second is not None, spread),
        (4,),
        info,
        inputs,
        one * (len(inputs) // 2),
        outs,
        out_specs,
        [],
        1.2e9,
        "weight_grad",
    )
    if spread:
        return {(rx, ry): got[2 * rx + ry] for rx in (0, 1) for ry in (0, 1)}
    return got


def adam_step(master, moment, second, gradient, decay):
    moment_new = BETA_ONE * moment + (1.0 - BETA_ONE) * gradient
    second_new = BETA_TWO * second + (1.0 - BETA_TWO) * gradient * gradient
    rising = moment_new / (1.0 - BETA_ONE**STEP)
    spread = jnp.sqrt(second_new / (1.0 - BETA_TWO**STEP))
    return (moment_new, second_new, -LEARN_RATE * (rising / (spread + ADAM_EPS) + decay * master))


def describe(keys, from_row, count, shift):
    return [(key, from_row, count, shift) for key in keys]


def gather_weights(spread, qkv, out, up, down, layer):
    main = jnp.concatenate([qkv[layer, 0], qkv[layer, 1], qkv[layer, 2], out[layer].T], 1)
    main, up_low, down_low = main.astype(BF), up[layer].astype(BF), down[layer].T.astype(BF)
    if not spread:
        planes = []
        for own in (main, up_low, down_low):
            whole = lax.all_gather(own, "dp", axis=0, tiled=True)
            planes.append(([whole, swap_x(whole)], [(0,), (1,)]))
        return planes
    if layer == 0:
        left = gather_pieces(main[:48], "zxy")
        right = gather_pieces(main[48:], "zyx")
        ups = gather_pieces(up_low, "zxy")
        downs = gather_pieces(down_low, "zyx")
        return [
            (left + right, describe(KEYS, 0, 48, 0) + describe(KEYS, 0, 48, 48)),
            (ups, describe(KEYS, 0, 96, 0)),
            (downs, describe(KEYS, 0, 96, 0)),
        ]
    left = gather_pieces(jnp.concatenate([main[:48], up_low], 0), "zxy")
    right = gather_pieces(jnp.concatenate([main[48:], down_low], 0), "zyx")
    return [
        (left + right, describe(KEYS, 0, 48, 0) + describe(KEYS, 0, 48, 48)),
        (left, describe(KEYS, 48, 96, 0)),
        (right, describe(KEYS, 48, 96, 0)),
    ]


def sum_everywhere(spread, rows):
    turned = jnp.concatenate([rows[:, :3], rows[:, 4:5], rows[:, 3:4], rows[:, 5:]], 1)
    rows = rows + swap_x(turned)
    if not spread:
        return lax.psum(rows, "dp")
    for bit in (1, 2, 4):
        rows = rows + swap(rows, "dp", bit)
    return rows


def body(
    query_tokens,
    passage_tokens,
    query_mask,
    passage_lengths,
    positives,
    qkv_weight,
    qkv_moment,
    qkv_second,
    out_weight,
    out_moment,
    out_second,
    up_weight,
    up_moment,
    up_second,
    down_weight,
    down_moment,
    down_second,
    projection,
    projection_moment,
    projection_second,
    bias_pair,
    bias_pair_moment,
    bias_pair_second,
    bias_up,
    bias_up_moment,
    bias_up_second,
    norm_terms,
    norm_terms_moment,
    norm_terms_second,
):
    groups = lax.axis_size("dp")
    spread = groups == 8
    tensor_at = lax.axis_index("tensor")
    which_x, core = tensor_at // 2, tensor_at % 2
    group = lax.axis_index("dp")
    blocks = 4 if spread else 1
    first_block = 4 * core if spread else group
    info = jnp.stack(
        [which_x, group % 2, group // 2, core, group, first_block, group * 0, group * 0]
    ).astype(jnp.int32)
    on_left = which_x == 0

    planes = [
        gather_weights(spread, qkv_weight, out_weight, up_weight, down_weight, layer)
        for layer in range(LAYERS)
    ]
    proj_low = projection.astype(BF)
    if spread:
        proj = (
            gather_pieces(proj_low, "zy", use_x=False),
            describe(PLAIN_KEYS, 0, 96, 0),
        )
    else:
        proj = ([lax.all_gather(proj_low, "dp", axis=0, tiled=True)], [(0,)])
    small = jnp.concatenate([bias_pair[:, 0], bias_pair[:, 1], bias_up], 1)
    smalls = (small, swap_x(small))
    nothing = jnp.zeros((PART,), F32)
    biases = [
        jnp.stack(
            [
                jnp.concatenate([s[layer, :PART], nothing, s[layer, PART : 2 * PART], nothing])
                for s in smalls
            ]
        )
        for layer in range(LAYERS)
    ]
    biases_up = [
        jnp.stack([s[layer, 2 * PART :] for s in smalls]) for layer in range(LAYERS)
    ]

    states = jnp.where(
        on_left,
        jnp.concatenate([query_tokens, passage_tokens[:SEQ]], 0),
        passage_tokens[SEQ:],
    )
    key_at = lax.broadcasted_iota(jnp.int32, (SEQ, SEQ), 0)
    query_at = lax.broadcasted_iota(jnp.int32, (SEQ, SEQ), 1)
    own_lengths = lax.dynamic_slice_in_dim(passage_lengths, group * PDEV, PDEV, 0)
    valid_query = (key_at // QLEN == query_at // QLEN) & (query_mask.reshape(SEQ, 1) == 1)
    keep_first = jnp.where(on_left, valid_query, key_at < own_lengths[1])
    keep_second = key_at < jnp.where(on_left, own_lengths[0], own_lengths[2])
    masks = jnp.where(jnp.stack([keep_first, keep_second]), 0.0, MASKED).astype(F32)

    saved = []
    normed = None
    for layer in range(LAYERS):
        main, up, down = planes[layer]
        got = attention_forward(info, main, states, normed, biases[layer], masks)
        both, logs, xt, part = got[:4]
        if normed is not None:
            states = got[4]
            saved[-1] += [got[5], got[6]]
        first, normal_one, factor_one, first_t, pre, act, part = hidden_forward(
            info, up, down, states, part, swap_core(part), norm_terms[layer], biases_up[layer]
        )
        saved.append([both, logs, xt, normal_one, factor_one, first_t, pre, act])
        normed = (first, part, swap_core(part), norm_terms[layer])
    normal, factor, top_t, embedded, unit, unit_half, proj_full = embed(info, proj, *normed)
    saved[-1] += [normal, factor]

    if spread:
        pieces = gather_pieces(unit_half[:128], "zxy") + gather_pieces(unit_half[128:], "zyx")
        own = lay_out(info, pieces)
    else:
        whole = lax.all_gather(unit_half, "dp")
        other = swap_x(whole)
        own = jnp.where(on_left, jnp.stack([whole, other]), jnp.stack([other, whole]))
    everything, sums = score(info, passage_lengths, own, swap_core(own), blocks)
    log_lengths = jnp.log(passage_lengths.astype(F32))[:, None]
    smooth = (jnp.log(sums) - log_lengths) / SHARPNESS
    logits = SCORE_SCALE * jnp.sum(smooth.reshape(smooth.shape[0], blocks * QDEV, QLEN), -1)
    if spread:
        other = swap_core(logits)
        logits = jnp.where(
            core == 0, jnp.concatenate([logits, other], 1), jnp.concatenate([other, logits], 1)
        )
    else:
        logits = lax.all_gather(logits, "dp", axis=1, tiled=True)
    highest = jnp.max(logits, 0, keepdims=True)
    powers = jnp.exp(logits - highest)
    summed = jnp.sum(powers, 0, keepdims=True)
    chosen = lax.broadcasted_iota(jnp.int32, logits.shape, 0) == positives[None, :]
    losses = highest + jnp.log(summed) - jnp.sum(jnp.where(chosen, logits, 0.0), 0, keepdims=True)
    loss_mean = jnp.sum(losses) / logits.shape[1]
    steer = SCORE_SCALE * (powers / summed - chosen.astype(F32))
    steer = jnp.broadcast_to(steer[:, :, None], steer.shape + (QLEN,)).reshape(steer.shape[0], -1)
    upstream, proj_grad = score_back(
        info, passage_lengths, everything, steer, embedded, top_t, proj_full
    )

    upstreams = (upstream,)
    shards = []
    vectors = []
    for layer in range(LAYERS - 1, -1, -1):
        main, up, down = planes[layer]
        both, logs, xt, normal_one, factor_one, first_t, pre, act, normal_two, factor_two = saved[
            layer
        ]
        grad_two, low_t, pre_low, part, vec_two = hidden_backward(
            info, up, down, upstreams, normal_two, factor_two, norm_terms[layer], pre
        )
        other = swap_core(part)
        down_blocks = weight_grad(info, spread, low_t, act)
        up_blocks = weight_grad(info, spread, first_t, pre_low)
        grad_one, low_one_t, mixed, part, vec_one = attention_backward(
            info,
            main,
            grad_two,
            part,
            other,
            normal_one,
            factor_one,
            norm_terms[layer],
            both,
            logs,
            masks,
        )
        other = swap_core(part)
        main_blocks = weight_grad(info, spread, xt, mixed, (low_one_t, both))
        upstreams = (grad_one, part, other)
        if spread:
            shards.insert(
                0,
                (
                    reduce_blocks(main_blocks, "yx" if layer else "xy"),
                    reduce_blocks(up_blocks, "yx"),
                    reduce_blocks(down_blocks, "xy"),
                ),
            )
        else:
            shards.insert(
                0,
                tuple(
                    lax.psum_scatter(
                        b[0].astype(F32) + swap_x(b[1]).astype(F32), "dp", tiled=True
                    )
                    for b in (main_blocks, up_blocks, down_blocks)
                ),
            )
        vectors.insert(0, jnp.stack([vec_one, vec_two]))

    if spread:
        shaped = proj_grad.reshape(4, 2, 96, DIM)
        odd = group % 2 == 1
        keep = jnp.where(odd, shaped[:, 1], shaped[:, 0])
        send = jnp.where(odd, shaped[:, 0], shaped[:, 1]).astype(BF)
        line = keep + swap_y(send).astype(F32)
        z_at = group // 2
        total = lax.dynamic_index_in_dim(line, z_at, 0, False)
        for by in (1, 2, 3):
            block = lax.dynamic_index_in_dim(line, (z_at + by) % 4, 0, False).astype(BF)
            total = total + shift_z(block, by).astype(F32)
        projection_grad = total + swap_x(total)
    else:
        projection_grad = lax.psum_scatter(
            proj_grad + swap_x(proj_grad), "dp", scatter_dimension=0, tiled=True
        )

    vectors = [sum_everywhere(spread, rows) for rows in vectors]
    pair_grad = jnp.stack(
        [jnp.stack([v[0, 3, :PART], v[0, 3, 2 * PART : 3 * PART]]) for v in vectors]
    )
    bias_grad = jnp.stack([v[1, 3] for v in vectors])
    norms_grad = jnp.stack(
        [jnp.stack([v[0, 2], v[0, 0], v[0, 1], v[1, 2], v[1, 0], v[1, 1]]) for v in vectors]
    )

    whole = upstreams[0] + (upstreams[1].astype(F32) + upstreams[2].astype(F32))
    passed = swap_x(jnp.where(on_left, whole[128:256], whole[:128]).astype(BF)).astype(F32)
    query_rows = jnp.where(on_left, whole[:128], passed)
    passage_rows = jnp.where(on_left, jnp.concatenate([whole[SEQ:], passed], 0), whole[128:])
    query_grad = lax.dynamic_slice_in_dim(query_rows, core * 64, 64, 0)
    passage_grad = lax.dynamic_slice_in_dim(passage_rows, core * PART, PART, 0)

    qkv_grad = jnp.stack(
        [
            jnp.stack([s[0][:, at * PART : (at + 1) * PART] for at in range(3)])
            for s in shards
        ]
    )
    out_grad = jnp.stack([s[0][:, 3 * PART :].T for s in shards])
    up_grad = jnp.stack([s[1] for s in shards])
    down_grad = jnp.stack([s[2].T for s in shards])
    qkv_m, qkv_v, qkv_u = adam_step(qkv_weight, qkv_moment, qkv_second, qkv_grad, WEIGHT_DECAY)
    out_m, out_v, out_u = adam_step(out_weight, out_moment, out_second, out_grad, WEIGHT_DECAY)
    up_m, up_v, up_u = adam_step(up_weight, up_moment, up_second, up_grad, WEIGHT_DECAY)
    down_m, down_v, down_u = adam_step(
        down_weight, down_moment, down_second, down_grad, WEIGHT_DECAY
    )
    proj_m, proj_v, proj_u = adam_step(
        projection, projection_moment, projection_second, projection_grad, WEIGHT_DECAY
    )
    pair_m, pair_v, pair_u = adam_step(
        bias_pair, bias_pair_moment, bias_pair_second, pair_grad, 0.0
    )
    bias_m, bias_v, bias_u = adam_step(bias_up, bias_up_moment, bias_up_second, bias_grad, 0.0)
    norm_m, norm_v, norm_u = adam_step(
        norm_terms, norm_terms_moment, norm_terms_second, norms_grad, 0.0
    )
    return (
        loss_mean,
        query_grad,
        passage_grad,
        qkv_grad,
        qkv_m,
        qkv_v,
        qkv_u,
        out_grad,
        out_m,
        out_v,
        out_u,
        up_grad,
        up_m,
        up_v,
        up_u,
        down_grad,
        down_m,
        down_v,
        down_u,
        projection_grad,
        proj_m,
        proj_v,
        proj_u,
        pair_grad,
        pair_m,
        pair_v,
        pair_u,
        bias_grad,
        bias_m,
        bias_v,
        bias_u,
        norms_grad,
        norm_m,
        norm_v,
        norm_u,
    )


def solution(mesh):
    rows = P("dp", None)
    qkv, out, up = P(None, None, "dp", "tensor"), P(None, "tensor", "dp"), P(None, "dp", "tensor")
    pair, wide = P(None, None, "tensor"), P(None, "tensor")
    placed = (
        (rows, rows, rows, P(), P())
        + (qkv,) * 3
        + (out,) * 3
        + (up,) * 3
        + (out,) * 3
        + (rows,) * 3
        + (pair,) * 3
        + (wide,) * 3
        + (P(),) * 3
    )
    both = P(("dp", "tensor"), None)
    given = (
        (P(), both, both)
        + (qkv,) * 4
        + (out,) * 4
        + (up,) * 4
        + (out,) * 4
        + (rows,) * 4
        + (pair,) * 4
        + (wide,) * 4
        + (P(),) * 4
    )
    return jax.shard_map(body, mesh=mesh, in_specs=placed, out_specs=given, check_vma=False)
```
